32 devices in a mesh: grp: 2 (over y), gx: 4 (over z), gy: 2 (over x), row: 2 (over core).
Axes of the slice: x: 2, y: 2, z: 4, core: 2. Of those that a mesh axis runs over, the one named last changes fastest.
Arguments:
- conc: float32 [64, 8, 16, 128], P(None, ('grp', 'gx'), ('gy', 'row')), parts along dimension 1, may hold values from 0.2 to 2
- cotangent: float32 [64, 8, 16, 128], P(None, ('grp', 'gx'), ('gy', 'row')), parts along dimension 1, may hold values from -6 to 6
- courant: float32 [32, 128], P(('grp', 'gy', 'row')), parts along dimension 0, may hold values from 8 to 100
- direction: int32 [32, 128], P(('grp', 'gy', 'row')), parts along dimension 0, may hold values 0 or 1
- rate_const: float32 [1024], replicated, may hold values from 0.01 to 0.1
- orders: int32 [1024, 64], replicated, may hold values from 0 to 2, as said below
- stoich: int32 [64, 1024], replicated, may hold values from -2 to 1, as said below
Outputs:
- final_state: float32 [64, 8, 16, 128], P(None, ('grp', 'gx'), ('gy', 'row')), parts along dimension 1
- adjoint: float32 [64, 8, 16, 128], P(None, ('grp', 'gx'), ('gy', 'row')), parts along dimension 1
The draws below stay inside these ranges and needn't reach their ends.
There are 2 independent parts, one for each index of `grp`. The reference program is written for one: setup_inputs(seed, part) draws one part's arguments, and reference() takes and returns one part's arrays. A program takes and returns all parts, laid end to end along the dimension named above; an argument that names none is the same for every part. Nothing has to cross between parts.
Inputs may be any that keep to these rules, and one draw needn't show every extreme that they name: `orders`: each reaction has two different reactants, each of order 1 or 2, and no other nonzero order. stoich[s, j] is 1 for the product species of reaction j (one species) minus orders[j, s].
All inputs are finite; a program needn't handle non-finite values. No bound on the sum of `direction` on one device may be relied on, other than what follows from the above.
Results may differ from the reference program's by a relative error of at most 0.0003.
Values sent between devices are 32-bit elements; how exact they have to be, the bound alone decides.
A program may use at most 64 MiB of HBM per device.

```python
import math
import jax
import jax.numpy as jnp
from jax import lax

S = 64
R = 1024
NZ = 128
STEPS = 2
NX = 4
NY = 16


def reaction_table(key):
    base = jax.random.fold_in(key, 11)
    key_one, key_two, key_three, key_four, key_five = jax.random.split(base, 5)
    reactant_one = jax.random.randint(key_one, (R,), 0, S)
    reactant_two = (reactant_one + jax.random.randint(key_two, (R,), 1, S)) % S
    product = jax.random.randint(key_three, (R,), 0, S)
    order_one = jax.random.randint(key_four, (R,), 1, 3)
    order_two = jax.random.randint(key_five, (R,), 1, 3)
    species = jnp.arange(S, dtype=jnp.int32)[None, :]
    orders = (species == reactant_one[:, None]).astype(jnp.int32) * order_one[:, None]
    orders = orders + (species == reactant_two[:, None]).astype(jnp.int32) * order_two[:, None]
    stoich = (species == product[:, None]).astype(jnp.int32) - orders
    return (orders, stoich.T)


def draw_orders(key, part):
    return reaction_table(key)[0]


def draw_stoich(key, part):
    return reaction_table(key)[1]


def touch_ends(entries, rng, smallest, largest):
    spot = [jax.random.randint(jax.random.fold_in(rng, axis), (), 0, length) for axis, length in enumerate(entries.shape)]
    main_axis = entries.shape.index(max(entries.shape))
    beside = spot[:main_axis] + [(spot[main_axis] + 1) % entries.shape[main_axis]] + spot[main_axis + 1:]
    return entries.at[tuple(spot)].set(smallest).at[tuple(beside)].set(largest)


def steps_of(rng, shape, cuts, least, high):
    level, own = 1.0, jax.random.fold_in(rng, 6)
    for axis_at, shards_of in cuts:
        heights = jnp.exp(jax.random.uniform(jax.random.fold_in(own, axis_at), (shards_of,), jnp.float32, least / len(cuts), high / len(cuts)))
        level = level * jnp.repeat(heights, shape[axis_at] // shards_of).reshape([-1 if axis == axis_at else 1 for axis in range(len(shape))])
    return level


def gaussian(key, dims, width, bound, cuts=(), kind=jnp.bfloat16):
    loudness = steps_of(key, dims, cuts, -0.22, 0.18) if cuts else 1.0
    entries = jax.random.normal(key, dims, jnp.float32) * width * loudness
    return jnp.minimum(jnp.maximum(entries, -bound), bound).astype(kind)


def setup_inputs(seed: int = 0, part: int = 0) -> dict:
    key_list = jax.random.split(jax.random.key(seed), 8)
    part_keys = jax.random.split(jax.random.fold_in(key_list[7], part), 8)
    conc = jnp.clip(0.2 + 1.8 * jax.random.uniform(part_keys[0], (S, NX, NY, NZ), jnp.float32) ** steps_of(part_keys[0], (S, NX, NY, NZ), ((1, 4), (2, 4)), -0.2, 0.2), 0.2, 2.0)
    cotangent = gaussian(part_keys[1], (S, NX, NY, NZ), 1.0, 6.0, ((1, 4), (2, 4)), jnp.float32)
    courant = jnp.clip(jnp.exp(math.log(100.0) - 2.5257286 * jax.random.uniform(part_keys[2], (NY, NZ), jnp.float32) ** steps_of(part_keys[2], (NY, NZ), ((0, 4),), -0.2, 0.2)), 8.0, 100.0)
    direction = touch_ends((jax.random.randint(part_keys[3], (NY, NZ), 0, 2) < 1).astype(jnp.int32), jax.random.fold_in(part_keys[3], 1), 0, 1)
    rate_const = jnp.clip(jnp.exp(jax.random.uniform(key_list[4], (R,), jnp.float32, math.log(0.01), math.log(0.1))), 0.01, 0.1)
    orders = draw_orders(jax.random.fold_in(key_list[7], 71), part)
    stoich = draw_stoich(jax.random.fold_in(key_list[7], 71), part)
    return dict(conc=conc, cotangent=cotangent, courant=courant, direction=direction, rate_const=rate_const, orders=orders, stoich=stoich)


time_step = 0.1
diffusion = 0.1
highest = lax.Precision.HIGHEST


def combine_pairs(leading, trailing):
    return (leading[0] * trailing[0], trailing[0] * leading[1] + trailing[1])


def recurrence(values, weight, backward):
    multipliers = jnp.broadcast_to(weight[None, None], (1, values.shape[1]) + weight.shape)
    return lax.associative_scan(combine_pairs, (multipliers, values), reverse=backward, axis=1)


def sweep(values, weight, upward):
    rising = recurrence(values, weight, False)[1]
    falling = recurrence(values, weight, True)[1]
    return jnp.where(upward[None, None], rising, falling)


def smooth(values):
    padded = jnp.pad(values, ((0, 0), (0, 0), (1, 1), (1, 1)))
    beside_all = padded[:, :, 2:, 1:-1] + padded[:, :, :-2, 1:-1] + padded[:, :, 1:-1, 2:] + padded[:, :, 1:-1, :-2]
    return values + diffusion * (beside_all - 4.0 * values)


def to_slices(values):
    return jnp.moveaxis(values.reshape(values.shape[0], values.shape[1], -1), 1, 0)


def from_slices(slices, shape):
    return jnp.moveaxis(slices, 0, 1).reshape(shape)


def reaction_rates(cells, order_float, rate_const):
    activity = 0.5 * jnp.log1p(cells * cells)
    return rate_const[:, None] * jnp.exp(jnp.dot(order_float, activity, precision=highest))


def reference(conc, cotangent, courant, direction, rate_const, orders, stoich):
    order_float = orders.astype(jnp.float32)
    stoich_float = stoich.astype(jnp.float32)
    retain = courant / (1.0 + courant)
    admit = 1.0 / (1.0 + courant)

    def react(cells):
        return cells + time_step * jnp.dot(stoich_float, reaction_rates(cells, order_float, rate_const), precision=highest)

    def react_back(paired):
        cells, spread = paired
        rates = reaction_rates(cells, order_float, rate_const)
        pulled = jnp.dot(stoich_float.T, spread, precision=highest)
        summed = jnp.dot(order_float.T, rates * pulled, precision=highest)
        return spread + time_step * cells / (1.0 + cells * cells) * summed

    states = [conc]
    for position in range(STEPS):
        current = states[-1]
        starred = from_slices(lax.map(react, to_slices(current)), current.shape)
        states.append(sweep(admit * smooth(starred), retain, direction == 1))
    adjoint = cotangent
    for position in reversed(range(STEPS)):
        carried = admit * sweep(adjoint, retain, direction == 0)
        spread = smooth(carried)
        adjoint = from_slices(lax.map(react_back, (to_slices(states[position]), to_slices(spread))), spread.shape)
    return states[-1], adjoint
```

```python
import functools

import jax
import jax.numpy as jnp
from jax import lax
from jax.experimental import pallas as pl
from jax.experimental.pallas import tpu as pltpu
from jax.sharding import PartitionSpec as P

MESH = pl.DeviceIdType.MESH
F32 = jnp.float32
BF16 = jnp.bfloat16
TIME_STEP = 0.1
DIFFUSION = 0.1
HALF_LOG2E = 0.5 * 1.4426950408889634
FWD0, ADJ1, FWD1, ADJ0 = range(4)


def kernel(
    sizes, conc_hbm, cot_hbm, cour_ref, dir_ref, const_ref, ord_hbm, sto_hbm, fin_hbm, adj_hbm,
    conc, cot, state, spread, field, values, recv, sent, halo, out_fin, out_adj, rates0, rates_b, grad_b,
    ord_i, sto_i, ord2, ord_t, sto2, sto, log_k,
    in_sem, tab_sem, out_sem, send_sem, recv_sem, hsend_sem, hrecv_sem,
):
    nx, ngy, nrow = sizes
    ny = ngy * nrow
    depth, species, width = conc.shape
    reactions = ord_i.shape[1]
    edges = sorted({0, depth - 1})
    inner = list(range(1, depth - 1))
    groups = [g for g in (inner, edges) if g]
    order = [r for g in groups for r in g]
    chunk = min(256, reactions)

    x = lax.axis_index("gx")
    y = lax.axis_index("gy") * nrow + lax.axis_index("row")

    def line(target):
        return {"gy": lax.div(target, nrow), "row": lax.rem(target, nrow)}

    neighbours = [
        (x > 0, {"gx": x - 1}), (x < nx - 1, {"gx": x + 1}),
        (y > 0, line(y - 1)), (y < ny - 1, line(y + 1)),
    ]

    def load(item):
        source, target, base = item
        return [pltpu.make_async_copy(source.at[:, 0, r, :], target.at[r], in_sem.at[base, r]) for r in range(depth)]

    loads_cot = load((cot_hbm, cot, 0))
    loads_conc = load((conc_hbm, conc, 1))
    tables = [pltpu.make_async_copy(ord_hbm, ord_i, tab_sem.at[0]), pltpu.make_async_copy(sto_hbm, sto_i, tab_sem.at[1])]
    for copy in loads_cot + loads_conc + tables:
        copy.start()

    barrier = pltpu.get_barrier_semaphore()
    for there, device in neighbours:
        @pl.when(there)
        def _():
            pl.semaphore_signal(barrier, inc=1, device_id=device, device_id_type=MESH)

    @pl.when(x == 0)
    def _():
        for s in range(4):
            recv[s, 0] = jnp.zeros_like(recv[s, 0])

    @pl.when(x == nx - 1)
    def _():
        for s in range(4):
            recv[s, 1] = jnp.zeros_like(recv[s, 1])

    @pl.when(y == 0)
    def _():
        for s in range(4):
            halo[s, 0] = jnp.zeros_like(halo[s, 0])

    @pl.when(y == ny - 1)
    def _():
        for s in range(4):
            halo[s, 1] = jnp.zeros_like(halo[s, 1])

    courant = cour_ref[...]
    retain_all = courant / (1.0 + courant)
    admit_all = 1.0 / (1.0 + courant)
    retain = [retain_all[r:r + 1] for r in range(depth)]
    admit = [admit_all[r:r + 1] for r in range(depth)]
    rising = [jnp.broadcast_to(dir_ref[r:r + 1], (species, width)) for r in range(depth)]

    for copy in loads_cot:
        copy.wait()
    pl.semaphore_wait(barrier, sum(jnp.where(there, 1, 0) for there, _ in neighbours))

    one = jnp.where(x < (nx + 1) // 2, 0, 1)
    two = 1 - one

    def link(s, d, r):
        return pltpu.make_async_remote_copy(
            src_ref=sent.at[s, d, r], dst_ref=recv.at[s, d, r],
            send_sem=send_sem.at[s, d, r], recv_sem=recv_sem.at[s, d, r],
            device_id={"gx": x + 1 - 2 * d}, device_id_type=MESH,
        )

    def inside(position):
        return (position >= 0) & (position < nx)

    def relay(s, d, source, rows, arrive=True):
        pred, succ = inside(x - 1 + 2 * d), inside(x + 1 - 2 * d)
        for r in rows:
            if arrive:
                @pl.when(pred)
                def _():
                    link(s, d, r).wait_recv()
            sent[s, d, r] = source[r] + retain[r] * recv[s, d, r]

            @pl.when(succ)
            def _():
                link(s, d, r).start()

    first_end = jnp.logical_not(inside(x - 1 + 2 * one))

    def seed(s, source, rows):
        @pl.when(first_end)
        def _():
            relay(s, one, source, rows, arrive=False)

    def relay_first(s, source, rows):
        @pl.when(jnp.logical_not(first_end))
        def _():
            relay(s, one, source, rows)

    def chosen(s, r, adjoint):
        pick = (rising[r] == 0) if adjoint else (rising[r] == 1)
        return jnp.where(pick, sent[s, 0, r], sent[s, 1, r])

    def halo_copies(s):
        down = pltpu.make_async_remote_copy(
            src_ref=field.at[s, 0], dst_ref=halo.at[s, 1], send_sem=hsend_sem.at[s, 0], recv_sem=hrecv_sem.at[s, 1],
            device_id=line(y - 1), device_id_type=MESH)
        up = pltpu.make_async_remote_copy(
            src_ref=field.at[s, depth - 1], dst_ref=halo.at[s, 0], send_sem=hsend_sem.at[s, 1], recv_sem=hrecv_sem.at[s, 0],
            device_id=line(y + 1), device_id_type=MESH)
        return down, up

    def halo_send(s):
        @pl.when(y > 0)
        def _():
            halo_copies(s)[0].start()

        @pl.when(y < ny - 1)
        def _():
            halo_copies(s)[1].start()

    def halo_wait(s):
        @pl.when(y > 0)
        def _():
            halo_copies(s)[1].wait_recv()

        @pl.when(y < ny - 1)
        def _():
            halo_copies(s)[0].wait_recv()

    lane = lax.broadcasted_iota(jnp.int32, (species, width), 1)

    def smooth(s, r):
        here = field[s, r]
        below = halo[s, 0] if r == 0 else field[s, r - 1]
        above = halo[s, 1] if r == depth - 1 else field[s, r + 1]
        before = jnp.where(lane == 0, 0.0, pltpu.roll(here, 1, 1))
        after = jnp.where(lane == width - 1, 0.0, pltpu.roll(here, width - 1, 1))
        return here + DIFFUSION * (above + below + after + before - 4.0 * here)

    def side(parts):
        return parts[0] if len(parts) == 1 else jnp.concatenate(parts, axis=1)

    def split(value):
        high = value.astype(BF16)
        low = (value - high.astype(F32)).astype(BF16)
        return jnp.concatenate([high, low], axis=0)

    def activity(rows, source):
        return split(side([HALF_LOG2E * jnp.log(1.0 + source[r] * source[r]) for r in rows]))

    def rates_at(part, act, count):
        exponent = jnp.dot(ord2[part, :], act, preferred_element_type=F32)
        return jnp.exp2(exponent + side([log_k[part, :]] * count))

    parts = [pl.ds(i, chunk) for i in range(0, reactions, chunk)]

    def keep(target, part, cols, value):
        high = value.astype(BF16)
        target[0, part, cols] = high
        target[1, part, cols] = (value - high.astype(F32)).astype(BF16)

    def gather(table, halves, cols):
        small = jnp.dot(table[...], halves[1, :, cols], preferred_element_type=F32)
        return small + jnp.dot(table[...], halves[0, :, cols], preferred_element_type=F32)

    def columns(rows):
        start = order.index(rows[0]) * width
        return pl.ds(start, len(rows) * width)

    def put_react(rows, source, s, produced):
        for i, r in enumerate(rows):
            field[s, r] = source[r] + TIME_STEP * produced[:, i * width:(i + 1) * width]

    def react_first(rows):
        act, cols = activity(rows, conc), columns(rows)
        for part in parts:
            rates = rates_at(part, act, len(rows))
            rates0[part, cols] = rates
            keep(rates_b, part, cols, rates)
        put_react(rows, conc, FWD0, gather(sto, rates_b, cols))

    def put_back(rows, cells, summed, target):
        for i, r in enumerate(rows):
            c = cells[r]
            target[r] = spread[r] + TIME_STEP * c / (1.0 + c * c) * summed[:, i * width:(i + 1) * width]

    def react_both(rows):
        act, cols = activity(rows, state), columns(rows)
        push = split(side([spread[r] for r in rows]))
        for part in parts:
            rates = rates_at(part, act, len(rows))
            pulled = jnp.dot(sto2[part, :], push, preferred_element_type=F32)
            keep(rates_b, part, cols, rates)
            keep(grad_b, part, cols, rates * pulled)
        put_back(rows, state, gather(ord_t, grad_b, cols), values.at[1])
        seed(ADJ0, values.at[1], rows)
        put_react(rows, state, FWD1, gather(sto, rates_b, cols))

    def react_last(rows):
        cols = columns(rows)
        push = split(side([spread[r] for r in rows]))
        for part in parts:
            pulled = jnp.dot(sto2[part, :], push, preferred_element_type=F32)
            keep(grad_b, part, cols, rates0[part, cols] * pulled)
        put_back(rows, conc, gather(ord_t, grad_b, cols), out_adj)

    seed(ADJ1, cot, order)
    for copy in tables + loads_conc:
        copy.wait()
    order_float = ord_i[...].astype(F32)
    ord_t[...] = order_float.astype(BF16)
    order_trans = order_float.T.astype(BF16)
    ord2[:, :species] = order_trans
    ord2[:, species:] = order_trans
    stoich_float = sto_i[...].astype(F32)
    sto[...] = stoich_float.astype(BF16)
    stoich_trans = stoich_float.T.astype(BF16)
    sto2[:, :species] = stoich_trans
    sto2[:, species:] = stoich_trans
    log_k[...] = jnp.broadcast_to(jnp.log(const_ref[...]) * (2.0 * HALF_LOG2E), (width, reactions)).T

    react_first(edges)
    halo_send(FWD0)
    relay_first(ADJ1, cot, order)
    if inner:
        react_first(inner)

    def advance(s, source, rows):
        for r in rows:
            source[r] = admit[r] * smooth(s, r)
        seed(s, source, rows)

    advance(FWD0, values.at[0], inner)
    halo_wait(FWD0)
    advance(FWD0, values.at[0], edges)
    relay(ADJ1, two, cot, order)
    for r in order:
        field[ADJ1, r] = admit[r] * chosen(ADJ1, r, True)
    halo_send(ADJ1)
    relay_first(FWD0, values.at[0], order)
    for r in inner:
        spread[r] = smooth(ADJ1, r)
    halo_wait(ADJ1)
    for r in edges:
        spread[r] = smooth(ADJ1, r)
    for rows in groups:
        relay(FWD0, two, values.at[0], rows)
    for rows in groups:
        for r in rows:
            state[r] = chosen(FWD0, r, False)
        react_both(rows)
    halo_send(FWD1)
    relay_first(ADJ0, values.at[1], order)
    advance(FWD1, values.at[2], inner)
    halo_wait(FWD1)
    advance(FWD1, values.at[2], edges)
    relay(ADJ0, two, values.at[1], order)
    for r in order:
        field[ADJ0, r] = admit[r] * chosen(ADJ0, r, True)
    halo_send(ADJ0)
    relay_first(FWD1, values.at[2], order)
    for r in inner:
        spread[r] = smooth(ADJ0, r)
    if inner:
        react_last(inner)
    relay(FWD1, two, values.at[2], order)

    def store(source, target, base, r):
        return pltpu.make_async_copy(source.at[r], target.at[:, 0, r, :], out_sem.at[base, r])

    for r in order:
        out_fin[r] = chosen(FWD1, r, False)
        store(out_fin, fin_hbm, 0, r).start()
    for r in inner:
        store(out_adj, adj_hbm, 1, r).start()
    halo_wait(ADJ0)
    for r in edges:
        spread[r] = smooth(ADJ0, r)
    react_last(edges)
    for r in edges:
        store(out_adj, adj_hbm, 1, r).start()

    for s in range(4):
        for d in range(2):
            @pl.when(inside(x + 1 - 2 * d))
            def _():
                for r in range(depth):
                    link(s, d, r).wait_send()

        @pl.when(y > 0)
        def _():
            halo_copies(s)[0].wait_send()

        @pl.when(y < ny - 1)
        def _():
            halo_copies(s)[1].wait_send()
    for r in range(depth):
        store(out_fin, fin_hbm, 0, r).wait()
        store(out_adj, adj_hbm, 1, r).wait()


def solution(mesh):
    sizes = (mesh.shape["gx"], mesh.shape["gy"], mesh.shape["row"])

    def shards(conc, cotangent, courant, direction, rate_const, orders, stoich):
        species, slabs, depth, width = conc.shape
        reactions = orders.shape[0]
        assert slabs == 1
        block = (depth, species, width)
        anywhere = pl.BlockSpec(memory_space=pl.ANY)
        in_hbm = pl.BlockSpec(memory_space=pltpu.HBM)
        vmem = pl.BlockSpec(memory_space=pltpu.VMEM)
        cells = depth * width
        dma = pltpu.SemaphoreType.DMA
        return pl.pallas_call(
            functools.partial(kernel, sizes),
            name="flame_adjoint",
            out_shape=[jax.ShapeDtypeStruct(conc.shape, F32)] * 2,
            in_specs=[in_hbm, in_hbm, vmem, vmem, vmem, in_hbm, in_hbm],
            out_specs=[anywhere, anywhere],
            scratch_shapes=[
                pltpu.VMEM(block, F32), pltpu.VMEM(block, F32), pltpu.VMEM(block, F32), pltpu.VMEM(block, F32),
                pltpu.VMEM((4,) + block, F32), pltpu.VMEM((3,) + block, F32),
                pltpu.VMEM((4, 2) + block, F32), pltpu.VMEM((4, 2) + block, F32), pltpu.VMEM((4, 2) + block[1:], F32),
                pltpu.VMEM(block, F32), pltpu.VMEM(block, F32),
                pltpu.VMEM((reactions, cells), F32), pltpu.VMEM((2, reactions, cells), BF16), pltpu.VMEM((2, reactions, cells), BF16),
                pltpu.VMEM((species, reactions), jnp.int32), pltpu.VMEM((species, reactions), jnp.int32),
                pltpu.VMEM((reactions, 2 * species), BF16), pltpu.VMEM((species, reactions), BF16),
                pltpu.VMEM((reactions, 2 * species), BF16), pltpu.VMEM((species, reactions), BF16),
                pltpu.VMEM((reactions, width), F32),
                dma((2, depth)), dma((2,)), dma((2, depth)),
                dma((4, 2, depth)), dma((4, 2, depth)), dma((4, 2)), dma((4, 2)),
            ],
            compiler_params=pltpu.CompilerParams(collective_id=0, has_side_effects=True, vmem_limit_bytes=67043328),
        )(conc, cotangent, courant, direction, rate_const.reshape(1, reactions), orders.T, stoich)

    placed = (
        P(None, ("grp", "gx"), ("gy", "row"), None),
        P(None, ("grp", "gx"), ("gy", "row"), None),
        P(("grp", "gy", "row"), None),
        P(("grp", "gy", "row"), None),
        P(),
        P(),
        P(),
    )
    return jax.shard_map(
        shards,
        mesh=mesh,
        in_specs=placed,
        out_specs=(P(None, ("grp", "gx"), ("gy", "row"), None),) * 2,
        check_vma=False,
    )
```

```python
import functools

import jax
import jax.numpy as jnp
from jax import lax
from jax.experimental import pallas as pl
from jax.experimental.pallas import tpu as pltpu
from jax.sharding import PartitionSpec as P

MESH = pl.DeviceIdType.MESH
F32 = jnp.float32
BF16 = jnp.bfloat16
TIME_STEP = 0.1
DIFFUSION = 0.1
HALF_LOG2E = 0.5 * 1.4426950408889634
FWD0, ADJ1, FWD1, ADJ0 = range(4)


def kernel(
    sizes, conc_hbm, cot_hbm, cour_ref, dir_ref, const_ref, ord_hbm, sto_hbm, out_fin, out_adj,
    conc, cot, state, spread, field, values, recv, sent, halo, star, rates0, rates_b, grad_b,
    ord_i, sto_i, ord2, ord_t, sto2, sto, log_k,
    in_sem, tab_sem, send_sem, recv_sem, hsend_sem, hrecv_sem,
):
    nx, ngy, nrow = sizes
    ny = ngy * nrow
    depth, species, width = conc.shape
    reactions = ord_i.shape[1]
    edges = sorted({0, depth - 1})
    inner = list(range(1, depth - 1))
    groups = [g for g in (edges, inner) if g]
    order = [r for g in groups for r in g]
    chunk = min(256, reactions)
    pieces = send_sem.shape[3]
    piece = species // pieces

    x = lax.axis_index("gx")
    y = lax.axis_index("gy") * nrow + lax.axis_index("row")

    def line(target):
        return {"gy": lax.div(target, nrow), "row": lax.rem(target, nrow)}

    neighbours = [
        (x > 0, {"gx": x - 1}), (x < nx - 1, {"gx": x + 1}),
        (y > 0, line(y - 1)), (y < ny - 1, line(y + 1)),
    ]

    def load(item):
        source, target, base = item
        return [pltpu.make_async_copy(source.at[:, 0, r, :], target.at[r], in_sem.at[base, r]) for r in range(depth)]

    loads_cot = load((cot_hbm, cot, 0))
    loads_conc = load((conc_hbm, conc, 1))
    tables = [pltpu.make_async_copy(ord_hbm, ord_i, tab_sem.at[0]), pltpu.make_async_copy(sto_hbm, sto_i, tab_sem.at[1])]
    for copy in tables + loads_conc + loads_cot:
        copy.start()

    barrier = pltpu.get_barrier_semaphore()
    for there, device in neighbours:
        @pl.when(there)
        def _():
            pl.semaphore_signal(barrier, inc=1, device_id=device, device_id_type=MESH)

    @pl.when(x == 0)
    def _():
        for s in range(4):
            recv[s, 0] = jnp.zeros_like(recv[s, 0])

    @pl.when(x == nx - 1)
    def _():
        for s in range(4):
            recv[s, 1] = jnp.zeros_like(recv[s, 1])

    @pl.when(y == 0)
    def _():
        for s in range(4):
            halo[s, 0] = jnp.zeros_like(halo[s, 0])

    @pl.when(y == ny - 1)
    def _():
        for s in range(4):
            halo[s, 1] = jnp.zeros_like(halo[s, 1])

    courant = cour_ref[...]
    retain_all = courant / (1.0 + courant)
    admit_all = 1.0 / (1.0 + courant)
    retain = [retain_all[r:r + 1] for r in range(depth)]
    admit = [admit_all[r:r + 1] for r in range(depth)]
    rising = [jnp.broadcast_to(dir_ref[r:r + 1], (species, width)) for r in range(depth)]

    for copy in tables:
        copy.wait()
    order_float = ord_i[...].astype(F32)
    ord_t[...] = order_float.astype(BF16)
    order_trans = order_float.T.astype(BF16)
    ord2[:, :species] = order_trans
    ord2[:, species:] = order_trans
    stoich_float = sto_i[...].astype(F32)
    sto[...] = stoich_float.astype(BF16)
    stoich_trans = stoich_float.T.astype(BF16)
    sto2[:, :species] = stoich_trans
    sto2[:, species:] = stoich_trans
    log_k[...] = jnp.broadcast_to(jnp.log(const_ref[...]) * (2.0 * HALF_LOG2E), (width, reactions)).T
    for copy in loads_conc + loads_cot:
        copy.wait()
    pl.semaphore_wait(barrier, sum(jnp.where(there, 1, 0) for there, _ in neighbours))

    one = jnp.where(x < (nx + 1) // 2, 0, 1)
    two = 1 - one

    def link(s, d, r, h):
        part = pl.ds(h * piece, piece)
        return pltpu.make_async_remote_copy(
            src_ref=sent.at[s, d, r, part], dst_ref=recv.at[s, d, r, part],
            send_sem=send_sem.at[s, d, r, h], recv_sem=recv_sem.at[s, d, r, h],
            device_id={"gx": x + 1 - 2 * d}, device_id_type=MESH,
        )

    def inside(position):
        return (position >= 0) & (position < nx)

    def relay(s, d, source, rows, arrive=True):
        pred, succ = inside(x - 1 + 2 * d), inside(x + 1 - 2 * d)
        for r in rows:
            for h in range(pieces):
                part = pl.ds(h * piece, piece)
                if arrive:
                    @pl.when(pred)
                    def _():
                        link(s, d, r, h).wait_recv()
                sent[s, d, r, part] = source[r, part] + retain[r] * recv[s, d, r, part]

                @pl.when(succ)
                def _():
                    link(s, d, r, h).start()

    first_end = jnp.logical_not(inside(x - 1 + 2 * one))

    def seed(s, source, rows):
        @pl.when(first_end)
        def _():
            relay(s, one, source, rows, arrive=False)

    def relay_first(s, source, rows):
        @pl.when(jnp.logical_not(first_end))
        def _():
            relay(s, one, source, rows)

    def chosen(s, r, adjoint):
        pick = (rising[r] == 0) if adjoint else (rising[r] == 1)
        return jnp.where(pick, sent[s, 0, r], sent[s, 1, r])

    def halo_copies(s):
        source = conc if s == FWD0 else field.at[s]
        down = pltpu.make_async_remote_copy(
            src_ref=source.at[0], dst_ref=halo.at[s, 1], send_sem=hsend_sem.at[s, 0], recv_sem=hrecv_sem.at[s, 1],
            device_id=line(y - 1), device_id_type=MESH)
        up = pltpu.make_async_remote_copy(
            src_ref=source.at[depth - 1], dst_ref=halo.at[s, 0], send_sem=hsend_sem.at[s, 1], recv_sem=hrecv_sem.at[s, 0],
            device_id=line(y + 1), device_id_type=MESH)
        return down, up

    def halo_send(s):
        @pl.when(y > 0)
        def _():
            halo_copies(s)[0].start()

        @pl.when(y < ny - 1)
        def _():
            halo_copies(s)[1].start()

    def halo_wait(s):
        @pl.when(y > 0)
        def _():
            halo_copies(s)[1].wait_recv()

        @pl.when(y < ny - 1)
        def _():
            halo_copies(s)[0].wait_recv()

    lane = lax.broadcasted_iota(jnp.int32, (species, width), 1)

    def smooth(s, r):
        here = field[s, r]
        ends = star if s == FWD0 else halo.at[s]
        below = ends[0] if r == 0 else field[s, r - 1]
        above = ends[1] if r == depth - 1 else field[s, r + 1]
        before = jnp.where(lane == 0, 0.0, pltpu.roll(here, 1, 1))
        after = jnp.where(lane == width - 1, 0.0, pltpu.roll(here, width - 1, 1))
        return here + DIFFUSION * (above + below + after + before - 4.0 * here)

    def side(parts):
        return parts[0] if len(parts) == 1 else jnp.concatenate(parts, axis=1)

    def split(value):
        high = value.astype(BF16)
        low = (value - high.astype(F32)).astype(BF16)
        return jnp.concatenate([high, low], axis=0)

    def activity(rows, source):
        return split(side([HALF_LOG2E * jnp.log(1.0 + source[r] * source[r]) for r in rows]))

    def rates_at(part, act, count):
        exponent = jnp.dot(ord2[part, :], act, preferred_element_type=F32)
        return jnp.exp2(exponent + side([log_k[part, :]] * count))

    parts = [pl.ds(i, chunk) for i in range(0, reactions, chunk)]

    def keep(target, part, cols, value):
        high = value.astype(BF16)
        target[0, part, cols] = high
        target[1, part, cols] = (value - high.astype(F32)).astype(BF16)

    def gather(table, halves, cols):
        small = jnp.dot(table[...], halves[1, :, cols], preferred_element_type=F32)
        return small + jnp.dot(table[...], halves[0, :, cols], preferred_element_type=F32)

    def columns(rows):
        start = order.index(rows[0]) * width
        return pl.ds(start, len(rows) * width)

    def put_react(rows, source, s, produced):
        for i, r in enumerate(rows):
            field[s, r] = source[r] + TIME_STEP * produced[:, i * width:(i + 1) * width]

    def react_first(rows):
        act, cols = activity(rows, conc), columns(rows)
        for part in parts:
            rates = rates_at(part, act, len(rows))
            rates0[part, cols] = rates
            keep(rates_b, part, cols, rates)
        put_react(rows, conc, FWD0, gather(sto, rates_b, cols))

    def react_halo():
        act, cols = activity([0, 1], halo.at[FWD0]), pl.ds(0, 2 * width)
        for part in parts:
            keep(rates_b, part, cols, rates_at(part, act, 2))
        produced = gather(sto, rates_b, cols)
        for i, there in enumerate((y > 0, y < ny - 1)):
            value = halo[FWD0, i] + TIME_STEP * produced[:, i * width:(i + 1) * width]
            star[i] = jnp.where(there, value, 0.0)

    def put_back(rows, cells, summed, target):
        for i, r in enumerate(rows):
            c = cells[r]
            target[r] = spread[r] + TIME_STEP * c / (1.0 + c * c) * summed[:, i * width:(i + 1) * width]

    def react_both(rows):
        act, cols = activity(rows, state), columns(rows)
        push = split(side([spread[r] for r in rows]))
        for part in parts:
            rates = rates_at(part, act, len(rows))
            pulled = jnp.dot(sto2[part, :], push, preferred_element_type=F32)
            keep(rates_b, part, cols, rates)
            keep(grad_b, part, cols, rates * pulled)
        put_back(rows, state, gather(ord_t, grad_b, cols), values.at[1])
        seed(ADJ0, values.at[1], rows)
        put_react(rows, state, FWD1, gather(sto, rates_b, cols))

    def react_last(rows):
        cols = columns(rows)
        push = split(side([spread[r] for r in rows]))
        for part in parts:
            pulled = jnp.dot(sto2[part, :], push, preferred_element_type=F32)
            keep(grad_b, part, cols, rates0[part, cols] * pulled)
        put_back(rows, conc, gather(ord_t, grad_b, cols), out_adj)

    def advance(s, source, rows):
        for r in rows:
            source[r] = admit[r] * smooth(s, r)
        seed(s, source, rows)

    def arrive_back(s, source):
        for rows in groups:
            relay(s, two, source, rows)
            for r in rows:
                field[s, r] = admit[r] * chosen(s, r, True)
            if rows is groups[0]:
                halo_send(s)

    halo_send(FWD0)
    seed(ADJ1, cot, order)
    for rows in groups:
        react_first(rows)
    relay_first(ADJ1, cot, order)
    halo_wait(FWD0)
    react_halo()
    advance(FWD0, values.at[0], edges)
    advance(FWD0, values.at[0], inner)
    arrive_back(ADJ1, cot)
    relay_first(FWD0, values.at[0], order)
    for r in inner:
        spread[r] = smooth(ADJ1, r)
    halo_wait(ADJ1)
    for r in edges:
        spread[r] = smooth(ADJ1, r)
    for rows in groups:
        relay(FWD0, two, values.at[0], rows)
        for r in rows:
            state[r] = chosen(FWD0, r, False)
        react_both(rows)
        if rows is groups[0]:
            halo_send(FWD1)
    relay_first(ADJ0, values.at[1], order)
    advance(FWD1, values.at[2], inner)
    halo_wait(FWD1)
    advance(FWD1, values.at[2], edges)
    arrive_back(ADJ0, values.at[1])
    relay_first(FWD1, values.at[2], inner + edges)
    for r in inner:
        spread[r] = smooth(ADJ0, r)
    if inner:
        react_last(inner)
    relay(FWD1, two, values.at[2], inner + edges)
    for r in order:
        out_fin[r] = chosen(FWD1, r, False)
    halo_wait(ADJ0)
    for r in edges:
        spread[r] = smooth(ADJ0, r)
    react_last(edges)

    for s in range(4):
        for d in range(2):
            @pl.when(inside(x + 1 - 2 * d))
            def _():
                for r in range(depth):
                    for h in range(pieces):
                        link(s, d, r, h).wait_send()

        @pl.when(y > 0)
        def _():
            halo_copies(s)[0].wait_send()

        @pl.when(y < ny - 1)
        def _():
            halo_copies(s)[1].wait_send()


def solution(mesh):
    sizes = (mesh.shape["gx"], mesh.shape["gy"], mesh.shape["row"])

    def shards(conc, cotangent, courant, direction, rate_const, orders, stoich):
        species, slabs, depth, width = conc.shape
        reactions = orders.shape[0]
        assert slabs == 1
        block = (depth, species, width)
        in_hbm = pl.BlockSpec(memory_space=pltpu.HBM)
        vmem = pl.BlockSpec(memory_space=pltpu.VMEM)
        cells = depth * width
        dma = pltpu.SemaphoreType.DMA
        pieces = 2 if species % 16 == 0 else 1
        outs = pl.pallas_call(
            functools.partial(kernel, sizes),
            name="flame_adjoint",
            out_shape=[jax.ShapeDtypeStruct(block, F32)] * 2,
            in_specs=[in_hbm, in_hbm, vmem, vmem, vmem, in_hbm, in_hbm],
            out_specs=[vmem, vmem],
            scratch_shapes=[
                pltpu.VMEM(block, F32), pltpu.VMEM(block, F32), pltpu.VMEM(block, F32), pltpu.VMEM(block, F32),
                pltpu.VMEM((4,) + block, F32), pltpu.VMEM((3,) + block, F32),
                pltpu.VMEM((4, 2) + block, F32), pltpu.VMEM((4, 2) + block, F32), pltpu.VMEM((4, 2) + block[1:], F32),
                pltpu.VMEM((2,) + block[1:], F32),
                pltpu.VMEM((reactions, cells), F32), pltpu.VMEM((2, reactions, cells), BF16), pltpu.VMEM((2, reactions, cells), BF16),
                pltpu.VMEM((species, reactions), jnp.int32), pltpu.VMEM((species, reactions), jnp.int32),
                pltpu.VMEM((reactions, 2 * species), BF16), pltpu.VMEM((species, reactions), BF16),
                pltpu.VMEM((reactions, 2 * species), BF16), pltpu.VMEM((species, reactions), BF16),
                pltpu.VMEM((reactions, width), F32),
                dma((2, depth)), dma((2,)),
                dma((4, 2, depth, pieces)), dma((4, 2, depth, pieces)), dma((4, 2)), dma((4, 2)),
            ],
            compiler_params=pltpu.CompilerParams(collective_id=0, has_side_effects=True, vmem_limit_bytes=67043328),
        )(conc, cotangent, courant, direction, rate_const.reshape(1, reactions), orders.T, stoich)
        return tuple(out.transpose(1, 0, 2)[:, None] for out in outs)

    placed = (
        P(None, ("grp", "gx"), ("gy", "row"), None),
        P(None, ("grp", "gx"), ("gy", "row"), None),
        P(("grp", "gy", "row"), None),
        P(("grp", "gy", "row"), None),
        P(),
        P(),
        P(),
    )
    return jax.shard_map(
        shards,
        mesh=mesh,
        in_specs=placed,
        out_specs=(P(None, ("grp", "gx"), ("gy", "row"), None),) * 2,
        check_vma=False,
    )
```

```python
import functools

import jax
import jax.numpy as jnp
from jax import lax
from jax.experimental import pallas as pl
from jax.experimental.pallas import tpu as pltpu
from jax.sharding import PartitionSpec as P

MESH = pl.DeviceIdType.MESH
F32 = jnp.float32
BF16 = jnp.bfloat16
TIME_STEP = 0.1
DIFFUSION = 0.1
HALF_LOG2E = 0.5 * 1.4426950408889634
FWD0, ADJ1, FWD1, ADJ0 = range(4)


def kernel(
    sizes, conc_hbm, cot_hbm, cour_ref, dir_ref, const_ref, ord_hbm, sto_hbm, out_fin, out_adj,
    conc, cot, state, spread, field, values, recv, sent, halo, star, rates0, rates_b, grad_b,
    ord_i, sto_i, ord2, ord_t, sto2, sto, log_k,
    in_sem, tab_sem, send_sem, recv_sem, hsend_sem, hrecv_sem,
):
    nx, ngy, nrow = sizes
    ny = ngy * nrow
    depth, species, width = conc.shape
    reactions = ord_i.shape[1]
    edges = sorted({0, depth - 1})
    inner = list(range(1, depth - 1))
    groups = [g for g in (edges, inner) if g]
    order = [r for g in groups for r in g]
    chunk = min(256, reactions)
    pieces = send_sem.shape[3]
    piece = species // pieces

    x = lax.axis_index("gx")
    y = lax.axis_index("gy") * nrow + lax.axis_index("row")

    def line(target):
        return {"gy": lax.div(target, nrow), "row": lax.rem(target, nrow)}

    neighbours = [
        (x > 0, {"gx": x - 1}), (x < nx - 1, {"gx": x + 1}),
        (y > 0, line(y - 1)), (y < ny - 1, line(y + 1)),
    ]

    def load(item):
        source, target, base = item
        return [pltpu.make_async_copy(source.at[:, 0, r, :], target.at[r], in_sem.at[base, r]) for r in range(depth)]

    loads_cot = load((cot_hbm, cot, 0))
    loads_conc = load((conc_hbm, conc, 1))
    tables = [pltpu.make_async_copy(ord_hbm, ord_i, tab_sem.at[0]), pltpu.make_async_copy(sto_hbm, sto_i, tab_sem.at[1])]
    for copy in tables + loads_conc + loads_cot:
        copy.start()

    barrier = pltpu.get_barrier_semaphore()
    for there, device in neighbours:
        @pl.when(there)
        def _():
            pl.semaphore_signal(barrier, inc=1, device_id=device, device_id_type=MESH)

    @pl.when(x == 0)
    def _():
        for s in range(4):
            recv[s, 0] = jnp.zeros_like(recv[s, 0])

    @pl.when(x == nx - 1)
    def _():
        for s in range(4):
            recv[s, 1] = jnp.zeros_like(recv[s, 1])

    @pl.when(y == 0)
    def _():
        for s in range(4):
            halo[s, 0] = jnp.zeros_like(halo[s, 0])

    @pl.when(y == ny - 1)
    def _():
        for s in range(4):
            halo[s, 1] = jnp.zeros_like(halo[s, 1])

    courant = cour_ref[...]
    retain_all = courant / (1.0 + courant)
    admit_all = 1.0 / (1.0 + courant)
    retain = [retain_all[r:r + 1] for r in range(depth)]
    admit = [admit_all[r:r + 1] for r in range(depth)]
    rising = [jnp.broadcast_to(dir_ref[r:r + 1], (species, width)) for r in range(depth)]

    for copy in tables:
        copy.wait()
    order_float = ord_i[...].astype(F32)
    ord_t[...] = order_float.astype(BF16)
    order_trans = order_float.T.astype(BF16)
    ord2[:, :species] = order_trans
    ord2[:, species:] = order_trans
    stoich_float = sto_i[...].astype(F32)
    sto[...] = stoich_float.astype(BF16)
    stoich_trans = stoich_float.T.astype(BF16)
    sto2[:, :species] = stoich_trans
    sto2[:, species:] = stoich_trans
    log_k[...] = jnp.broadcast_to(jnp.log(const_ref[...]) * (2.0 * HALF_LOG2E), (width, reactions)).T
    for copy in loads_conc + loads_cot:
        copy.wait()
    pl.semaphore_wait(barrier, sum(jnp.where(there, 1, 0) for there, _ in neighbours))

    one = jnp.where(x < (nx + 1) // 2, 0, 1)
    two = 1 - one

    def link(s, d, r, h):
        part = pl.ds(h * piece, piece)
        return pltpu.make_async_remote_copy(
            src_ref=sent.at[s, d, r, part], dst_ref=recv.at[s, d, r, part],
            send_sem=send_sem.at[s, d, r, h], recv_sem=recv_sem.at[s, d, r, h],
            device_id={"gx": x + 1 - 2 * d}, device_id_type=MESH,
        )

    def inside(position):
        return (position >= 0) & (position < nx)

    def relay(s, d, source, rows, arrive=True):
        pred, succ = inside(x - 1 + 2 * d), inside(x + 1 - 2 * d)
        for r in rows:
            for h in range(pieces):
                part = pl.ds(h * piece, piece)
                if arrive:
                    @pl.when(pred)
                    def _():
                        link(s, d, r, h).wait_recv()
                sent[s, d, r, part] = source[r, part] + retain[r] * recv[s, d, r, part]

                @pl.when(succ)
                def _():
                    link(s, d, r, h).start()

    first_end = jnp.logical_not(inside(x - 1 + 2 * one))

    def seed(s, source, rows):
        @pl.when(first_end)
        def _():
            relay(s, one, source, rows, arrive=False)

    def relay_first(s, source, rows):
        @pl.when(jnp.logical_not(first_end))
        def _():
            relay(s, one, source, rows)

    def chosen(s, r, adjoint):
        pick = (rising[r] == 0) if adjoint else (rising[r] == 1)
        return jnp.where(pick, sent[s, 0, r], sent[s, 1, r])

    def halo_copies(s):
        source = conc if s == FWD0 else field.at[s]
        down = pltpu.make_async_remote_copy(
            src_ref=source.at[0], dst_ref=halo.at[s, 1], send_sem=hsend_sem.at[s, 0], recv_sem=hrecv_sem.at[s, 1],
            device_id=line(y - 1), device_id_type=MESH)
        up = pltpu.make_async_remote_copy(
            src_ref=source.at[depth - 1], dst_ref=halo.at[s, 0], send_sem=hsend_sem.at[s, 1], recv_sem=hrecv_sem.at[s, 0],
            device_id=line(y + 1), device_id_type=MESH)
        return down, up

    def halo_send(s):
        @pl.when(y > 0)
        def _():
            halo_copies(s)[0].start()

        @pl.when(y < ny - 1)
        def _():
            halo_copies(s)[1].start()

    def halo_wait(s):
        @pl.when(y > 0)
        def _():
            halo_copies(s)[1].wait_recv()

        @pl.when(y < ny - 1)
        def _():
            halo_copies(s)[0].wait_recv()

    lane = lax.broadcasted_iota(jnp.int32, (species, width), 1)

    def smooth(s, r):
        here = field[s, r]
        ends = star if s == FWD0 else halo.at[s]
        below = ends[0] if r == 0 else field[s, r - 1]
        above = ends[1] if r == depth - 1 else field[s, r + 1]
        before = jnp.where(lane == 0, 0.0, pltpu.roll(here, 1, 1))
        after = jnp.where(lane == width - 1, 0.0, pltpu.roll(here, width - 1, 1))
        return here + DIFFUSION * (above + below + after + before - 4.0 * here)

    def side(parts):
        return parts[0] if len(parts) == 1 else jnp.concatenate(parts, axis=1)

    def split(value):
        high = value.astype(BF16)
        low = (value - high.astype(F32)).astype(BF16)
        return jnp.concatenate([high, low], axis=0)

    def activity(rows, source):
        return split(side([HALF_LOG2E * jnp.log(1.0 + source[r] * source[r]) for r in rows]))

    def rates_at(part, act, count):
        exponent = jnp.dot(ord2[part, :], act, preferred_element_type=F32)
        return jnp.exp2(exponent + side([log_k[part, :]] * count))

    parts = [pl.ds(i, chunk) for i in range(0, reactions, chunk)]

    def keep(target, part, cols, value):
        high = value.astype(BF16)
        target[0, part, cols] = high
        target[1, part, cols] = (value - high.astype(F32)).astype(BF16)

    def gather(table, halves, cols):
        small = jnp.dot(table[...], halves[1, :, cols], preferred_element_type=F32)
        return small + jnp.dot(table[...], halves[0, :, cols], preferred_element_type=F32)

    def columns(rows):
        start = order.index(rows[0]) * width
        return pl.ds(start, len(rows) * width)

    def put_react(rows, source, s, produced):
        for i, r in enumerate(rows):
            field[s, r] = source[r] + TIME_STEP * produced[:, i * width:(i + 1) * width]

    def react_first(rows):
        act, cols = activity(rows, conc), columns(rows)
        for part in parts:
            rates = rates_at(part, act, len(rows))
            rates0[part, cols] = rates
            keep(rates_b, part, cols, rates)
        put_react(rows, conc, FWD0, gather(sto, rates_b, cols))

    def react_halo():
        act, cols = activity([0, 1], halo.at[FWD0]), pl.ds(0, 2 * width)
        for part in parts:
            keep(rates_b, part, cols, rates_at(part, act, 2))
        produced = gather(sto, rates_b, cols)
        for i, there in enumerate((y > 0, y < ny - 1)):
            value = halo[FWD0, i] + TIME_STEP * produced[:, i * width:(i + 1) * width]
            star[i] = jnp.where(there, value, 0.0)

    def put_back(rows, cells, summed, target):
        for i, r in enumerate(rows):
            c = cells[r]
            target[r] = spread[r] + TIME_STEP * c / (1.0 + c * c) * summed[:, i * width:(i + 1) * width]

    def react_both(rows):
        act, cols = activity(rows, state), columns(rows)
        push = split(side([spread[r] for r in rows]))
        for part in parts:
            rates = rates_at(part, act, len(rows))
            pulled = jnp.dot(sto2[part, :], push, preferred_element_type=F32)
            keep(rates_b, part, cols, rates)
            keep(grad_b, part, cols, rates * pulled)
        put_back(rows, state, gather(ord_t, grad_b, cols), values.at[1])
        seed(ADJ0, values.at[1], rows)
    def react_next(rows):
        put_react(rows, state, FWD1, gather(sto, rates_b, columns(rows)))

    def react_last(rows):
        cols = columns(rows)
        push = split(side([spread[r] for r in rows]))
        for part in parts:
            pulled = jnp.dot(sto2[part, :], push, preferred_element_type=F32)
            keep(grad_b, part, cols, rates0[part, cols] * pulled)
        put_back(rows, conc, gather(ord_t, grad_b, cols), out_adj)

    def advance(s, source, rows):
        for r in rows:
            source[r] = admit[r] * smooth(s, r)
        seed(s, source, rows)

    def arrive_back(s, source):
        for rows in groups:
            relay(s, two, source, rows)
            for r in rows:
                field[s, r] = admit[r] * chosen(s, r, True)
            if rows is groups[0]:
                halo_send(s)

    halo_send(FWD0)
    seed(ADJ1, cot, order)
    for rows in groups:
        react_first(rows)
    relay_first(ADJ1, cot, order)
    halo_wait(FWD0)
    react_halo()
    advance(FWD0, values.at[0], edges)
    advance(FWD0, values.at[0], inner)
    arrive_back(ADJ1, cot)
    relay_first(FWD0, values.at[0], order)
    for r in inner:
        spread[r] = smooth(ADJ1, r)
    halo_wait(ADJ1)
    for r in edges:
        spread[r] = smooth(ADJ1, r)
    for rows in groups:
        relay(FWD0, two, values.at[0], rows)
        for r in rows:
            state[r] = chosen(FWD0, r, False)
        react_both(rows)
    for rows in groups:
        react_next(rows)
        if rows is groups[0]:
            halo_send(FWD1)
    relay_first(ADJ0, values.at[1], order)
    advance(FWD1, values.at[2], inner)
    halo_wait(FWD1)
    advance(FWD1, values.at[2], edges)
    arrive_back(ADJ0, values.at[1])
    relay_first(FWD1, values.at[2], inner + edges)
    for r in inner:
        spread[r] = smooth(ADJ0, r)
    if inner:
        react_last(inner)
    relay(FWD1, two, values.at[2], inner + edges)
    for r in order:
        out_fin[r] = chosen(FWD1, r, False)
    halo_wait(ADJ0)
    for r in edges:
        spread[r] = smooth(ADJ0, r)
    react_last(edges)

    for s in range(4):
        for d in range(2):
            @pl.when(inside(x + 1 - 2 * d))
            def _():
                for r in range(depth):
                    for h in range(pieces):
                        link(s, d, r, h).wait_send()

        @pl.when(y > 0)
        def _():
            halo_copies(s)[0].wait_send()

        @pl.when(y < ny - 1)
        def _():
            halo_copies(s)[1].wait_send()


def solution(mesh):
    sizes = (mesh.shape["gx"], mesh.shape["gy"], mesh.shape["row"])

    def shards(conc, cotangent, courant, direction, rate_const, orders, stoich):
        species, slabs, depth, width = conc.shape
        reactions = orders.shape[0]
        assert slabs == 1
        block = (depth, species, width)
        in_hbm = pl.BlockSpec(memory_space=pltpu.HBM)
        vmem = pl.BlockSpec(memory_space=pltpu.VMEM)
        cells = depth * width
        dma = pltpu.SemaphoreType.DMA
        pieces = 2 if species % 16 == 0 else 1
        outs = pl.pallas_call(
            functools.partial(kernel, sizes),
            name="flame_adjoint",
            out_shape=[jax.ShapeDtypeStruct(block, F32)] * 2,
            in_specs=[in_hbm, in_hbm, vmem, vmem, vmem, in_hbm, in_hbm],
            out_specs=[vmem, vmem],
            scratch_shapes=[
                pltpu.VMEM(block, F32), pltpu.VMEM(block, F32), pltpu.VMEM(block, F32), pltpu.VMEM(block, F32),
                pltpu.VMEM((4,) + block, F32), pltpu.VMEM((3,) + block, F32),
                pltpu.VMEM((4, 2) + block, F32), pltpu.VMEM((4, 2) + block, F32), pltpu.VMEM((4, 2) + block[1:], F32),
                pltpu.VMEM((2,) + block[1:], F32),
                pltpu.VMEM((reactions, cells), F32), pltpu.VMEM((2, reactions, cells), BF16), pltpu.VMEM((2, reactions, cells), BF16),
                pltpu.VMEM((species, reactions), jnp.int32), pltpu.VMEM((species, reactions), jnp.int32),
                pltpu.VMEM((reactions, 2 * species), BF16), pltpu.VMEM((species, reactions), BF16),
                pltpu.VMEM((reactions, 2 * species), BF16), pltpu.VMEM((species, reactions), BF16),
                pltpu.VMEM((reactions, width), F32),
                dma((2, depth)), dma((2,)),
                dma((4, 2, depth, pieces)), dma((4, 2, depth, pieces)), dma((4, 2)), dma((4, 2)),
            ],
            compiler_params=pltpu.CompilerParams(collective_id=0, has_side_effects=True, vmem_limit_bytes=48 * 1024 * 1024),
        )(*[pltpu.with_memory_space_constraint(a, pltpu.HBM) for a in (conc, cotangent, courant, direction, rate_const.reshape(1, reactions), orders.T, stoich)])
        return tuple(out.transpose(1, 0, 2)[:, None] for out in outs)

    placed = (
        P(None, ("grp", "gx"), ("gy", "row"), None),
        P(None, ("grp", "gx"), ("gy", "row"), None),
        P(("grp", "gy", "row"), None),
        P(("grp", "gy", "row"), None),
        P(),
        P(),
        P(),
    )
    return jax.shard_map(
        shards,
        mesh=mesh,
        in_specs=placed,
        out_specs=(P(None, ("grp", "gx"), ("gy", "row"), None),) * 2,
        check_vma=False,
    )
```
